32 devices in a mesh: gx: 8 (over y, x, core), gy: 4 (over z).
Axes of the slice: x: 2, y: 2, z: 4, core: 2. Of those that a mesh axis runs over, the one named last changes fastest.
Arguments:
- modes: float32 [3, 64, 8192], P(None, None, ('gx', 'gy')), may hold values from -6 to 6
- weights: float32 [8192], P(('gx', 'gy')), may hold values from 0.25 to 4
Outputs:
- tensor: float32 [64, 64, 64], P('gx', 'gy')
The draws below stay inside these ranges and needn't reach their ends.
All inputs are finite; a program needn't handle non-finite values.
Results may differ from the reference program's by a relative error of at most 0.00018.
Values sent between devices are 32-bit elements; how exact they have to be, the bound alone decides.
A program may use at most 64 MiB of HBM per device.

```python
import math
import jax
import jax.numpy as jnp
from jax import lax

M = 64
NZ = 128
NX = 8
NY = 8
NCELLS = 8192


def steps_of(stream_key, shape, split, smallest, high):
    loudness, own = 1.0, jax.random.fold_in(stream_key, 6)
    for dim, shards_of in split:
        steps = jnp.exp(jax.random.uniform(jax.random.fold_in(own, dim), (shards_of,), jnp.float32, smallest / len(split), high / len(split)))
        loudness = loudness * jnp.repeat(steps, shape[dim] // shards_of).reshape([-1 if axis == dim else 1 for axis in range(len(shape))])
    return loudness


def bell_draw(key, shape, width, reach, split=(), kind=jnp.bfloat16):
    level = steps_of(key, shape, split, -0.22, 0.18) if split else 1.0
    values = jax.random.normal(key, shape, jnp.float32) * width * level
    return jnp.minimum(jnp.maximum(values, -reach), reach).astype(kind)


def setup_inputs(seed: int = 0) -> dict:
    key_list = jax.random.split(jax.random.key(seed), 3)
    return {
        "modes": bell_draw(key_list[0], (3, M, NCELLS), 1.0, 6.0, ((2, 32),), jnp.float32),
        "weights": jnp.clip(jnp.exp(math.log(4.0) - 2.7725887 * jax.random.uniform(key_list[1], (NCELLS,), jnp.float32) ** steps_of(key_list[1], (NCELLS,), ((0, 32),), -0.2, 0.2)), 0.25, 4.0),
    }


def differences(field, upper, lower):
    grad_x = (upper - lower) * 0.5
    grad_y = (jnp.roll(field, -1, axis=2) - jnp.roll(field, 1, axis=2)) * 0.5
    grad_z = (jnp.roll(field, -1, axis=3) - jnp.roll(field, 1, axis=3)) * 0.5
    return [grad_x, grad_y, grad_z]

def contribution(field, grads, weighted):
    weighted_field = field * weighted
    result = jnp.zeros((field.shape[1], field.shape[1], field.shape[1]), jnp.float32)
    for comp_a in range(3):
        inner = field[0][:, None, :] * grads[0][comp_a][None, :, :]
        inner = inner + field[1][:, None, :] * grads[1][comp_a][None, :, :]
        inner = inner + field[2][:, None, :] * grads[2][comp_a][None, :, :]
        result = result + jnp.einsum('ic,jkc->ijk', weighted_field[comp_a], inner, precision=lax.Precision.HIGHEST)
    return result

def reference(modes, weights):
    mode_count = modes.shape[1]
    grid = modes.reshape(3, mode_count, NZ, NY, NX).transpose(0, 1, 4, 3, 2)
    weight_grid = weights.reshape(NZ, NY, NX).transpose(2, 1, 0)
    factor = 1.0 / math.sqrt(NX * NY * NZ)
    padded = jnp.concatenate([grid[:, :, -1:], grid, grid[:, :, :1]], axis=2)

    def plane(total, position):
        slab = lax.dynamic_slice_in_dim(padded, position, 3, axis=2)
        field = slab[:, :, 1]
        grads = differences(field, slab[:, :, 2], slab[:, :, 0])
        weight_row = lax.dynamic_index_in_dim(weight_grid, position, 0, keepdims=False) * factor
        flat = field.reshape(3, mode_count, -1)
        flat_grads = [g.reshape(3, mode_count, -1) for g in grads]
        return (total + contribution(flat, flat_grads, weight_row.reshape(-1)), None)
    total, _ = lax.scan(plane, jnp.zeros((mode_count, mode_count, mode_count), jnp.float32), jnp.arange(NX, dtype=jnp.int32))
    return total
```

```python
import functools
import math

import jax
import jax.numpy as jnp
from jax import lax
from jax.experimental import pallas as pl
from jax.experimental.pallas import tpu as pltpu
from jax.sharding import PartitionSpec as P

CX = 1
CY = 2
LANES = 128
MESH = pl.DeviceIdType.MESH


def partner_of(gx):
    return gx + 1 - 2 * (gx % 2)


def split(value):
    high = value.astype(jnp.bfloat16)
    low = (value - high.astype(jnp.float32)).astype(jnp.bfloat16)
    return high, low


def kernel(
    nx, ny, modes, width, height, factor,
    x_ref, w_ref, out_ref,
    other_x, other_w, edges, halos, weighted, diffs, field2, high_h, low_h, sums, landed,
    near_send, near_recv, far_send, far_recv,
):
    rows, cells = x_ref.shape
    chips = nx // 2
    devices = nx * ny
    plane = width * height
    pack = max(1, LANES // plane)
    own_i = modes // nx
    own_j = modes // ny
    gx, gy = lax.axis_index("gx"), lax.axis_index("gy")
    core, place = gx % 2, gx // 2
    mate = (partner_of(gx), gy)
    flat = gx * ny + gy

    def beside(step, flat_id):
        other = (flat_id + step + devices) % devices
        return other // ny, other % ny

    def mated(device):
        return partner_of(device[0]), device[1]

    before, after = beside(-1, flat), beside(1, flat)
    mate_flat = mate[0] * ny + gy

    barrier = pltpu.get_barrier_semaphore()
    greeted = [mate, before, after, beside(-1, mate_flat), beside(1, mate_flat)]
    for s in range(chips):
        for t in range(ny):
            if s or t:
                greeted.append((((place + s) % chips) * 2 + core, (gy + t) % ny))
    for device in greeted:
        pl.semaphore_signal(barrier, inc=1, device_id=device, device_id_type=MESH)

    for edge, start in ((0, 0), (1, cells - plane)):
        if pack == 1:
            edges[edge] = x_ref[:, start : start + plane]
        else:
            base = start // LANES * LANES
            tile = x_ref[:, base : base + LANES]
            part = rows // pack
            lane = lax.broadcasted_iota(jnp.int32, (part, LANES), 1)
            packed = jnp.zeros((part, LANES), jnp.float32)
            for p in range(pack):
                shift = (p * plane - (start - base)) % LANES
                piece = tile[p * part : (p + 1) * part]
                piece = pltpu.roll(piece, shift, 1) if shift else piece
                packed = jnp.where(lane // plane == p, piece, packed)
            edges[edge] = packed

    pl.semaphore_wait(barrier, len(greeted))

    def near(index, src, dst, device):
        return pltpu.make_async_remote_copy(
            src_ref=src, dst_ref=dst, send_sem=near_send.at[index], recv_sem=near_recv.at[index],
            device_id=device, device_id_type=MESH,
        )

    copies = [
        near(0, edges.at[1], halos.at[0], after),
        near(1, edges.at[0], halos.at[1], before),
        near(2, edges.at[1], halos.at[2], mated(after)),
        near(3, edges.at[0], halos.at[3], mated(before)),
        near(4, w_ref, other_w, mate),
        near(5, x_ref, other_x, mate),
    ]
    for copy in copies:
        copy.start()

    lane = lax.broadcasted_iota(jnp.int32, (modes, cells), 1)
    at_x, at_y = lane % width, lane // width % height

    def rolled(value, step):
        shift = (-step) % cells
        return pltpu.roll(value, shift, 1) if shift else value

    def plane_of(slot, a):
        if pack == 1:
            tile = halos[slot, a * modes : (a + 1) * modes, :]
        else:
            tiles = []
            part = rows // pack
            narrow = lax.broadcasted_iota(jnp.int32, (8, LANES), 1)
            for r in range(a * modes, (a + 1) * modes, 8):
                p, q = r // part, r % part
                piece = halos[slot, q : q + 8, :]
                full = piece
                for m in range(1, pack):
                    full = jnp.where(narrow // plane == (p + m) % pack, pltpu.roll(piece, m * plane, 1), full)
                tiles.append(full)
            tile = jnp.concatenate(tiles, axis=0)
        return jnp.concatenate([tile] * (cells // tile.shape[1]), axis=1)

    def prepare(which, ref, weight_ref):
        columns = slice(which * cells, (which + 1) * cells)
        weight = weight_ref[...] * factor
        for a in range(3):
            value = ref[a * modes : (a + 1) * modes, :]
            for g in range(nx):
                weighted[g, a, :, columns] = value[g * own_i : (g + 1) * own_i] * weight
            high, low = split(value)
            field2[:modes, a * 2 * cells + which * cells : a * 2 * cells + (which + 1) * cells] = high
            field2[modes:, a * 2 * cells + which * cells : a * 2 * cells + (which + 1) * cells] = low
            up = jnp.where(at_x == width - 1, rolled(value, 1 - width), rolled(value, 1))
            down = jnp.where(at_x == 0, rolled(value, width - 1), rolled(value, -1))
            diffs[a, 0, :, columns] = (up - down) * 0.5
            turn = (height - 1) * width
            up = jnp.where(at_y == height - 1, rolled(value, -turn), rolled(value, width))
            down = jnp.where(at_y == 0, rolled(value, turn), rolled(value, -width))
            diffs[a, 1, :, columns] = (up - down) * 0.5

    def prepare_z(which, ref):
        columns = slice(which * cells, (which + 1) * cells)
        for a in range(3):
            value = ref[a * modes : (a + 1) * modes, :]
            up = jnp.where(lane >= cells - plane, plane_of(2 * which + 1, a), rolled(value, plane))
            down = jnp.where(lane < plane, plane_of(2 * which, a), rolled(value, -plane))
            diffs[a, 2, :, columns] = (up - down) * 0.5

    prepare(0, x_ref, w_ref)
    copies[4].wait_recv()
    copies[5].wait_recv()
    prepare(1, other_x, other_w)
    for copy in copies[:4]:
        copy.wait_recv()
    prepare_z(0, x_ref)
    prepare_z(1, other_x)

    both = 2 * cells
    me = place * ny + gy

    def far(s, t):
        to_place, to_gy = (place + s) % chips, (gy + t) % ny
        index = s * ny + t
        return pltpu.make_async_remote_copy(
            src_ref=sums.at[s, pl.ds(pl.multiple_of(to_gy * own_j, own_j), own_j), :],
            dst_ref=landed.at[me],
            send_sem=far_send.at[index], recv_sem=far_recv.at[me],
            device_id=(to_place * 2 + core, to_gy), device_id_type=MESH,
        )

    def block(s):
        group = (place + s) % chips * 2 + core
        for b in range(3):
            for c in range(0, both, LANES):
                tiles = [diffs[a, b, :, c : c + LANES] for a in range(3)]
                scales = [weighted[group, a, :, c : c + LANES] for a in range(3)]
                for i in range(own_i):
                    value = scales[0][i : i + 1] * tiles[0]
                    for a in (1, 2):
                        value = value + scales[a][i : i + 1] * tiles[a]
                    high, low = split(value)
                    place_of = slice(i * modes, (i + 1) * modes), slice(b * both + c, b * both + c + LANES)
                    high_h[place_of] = high
                    low_h[place_of] = low
        dims = (((1,), (1,)), ((), ()))
        main = lax.dot_general(field2[...], high_h[...], dims, preferred_element_type=jnp.float32)
        rest = lax.dot_general(field2[:modes, :], low_h[...], dims, preferred_element_type=jnp.float32)
        sums[s] = main[:modes] + (main[modes:] + rest)

    def step(index, carry):
        s = chips - 1 - index
        block(s)
        for t in range(ny - 1, 0, -1):
            far(s, t).start()

        @pl.when(s > 0)
        def _():
            far(s, 0).start()

        return carry

    lax.fori_loop(0, chips, step, 0)
    landed[me] = sums[0, pl.ds(pl.multiple_of(gy * own_j, own_j), own_j), :]
    for s in range(chips):
        for t in range(ny):
            if s or t:
                source = (place + s) % chips * ny + (gy + t) % ny
                pltpu.make_async_remote_copy(
                    src_ref=landed.at[source], dst_ref=landed.at[source],
                    send_sem=far_send.at[0], recv_sem=far_recv.at[source],
                    device_id=mate, device_id_type=MESH,
                ).wait_recv()
    total = landed[0]
    for q in range(1, chips * ny):
        total = total + landed[q]
    for i in range(own_i):
        out_ref[i] = total[:, i * modes : (i + 1) * modes]
    for copy in copies:
        copy.wait_send()
    for s in range(chips):
        for t in range(ny):
            if s or t:
                far(s, t).wait_send()


def per_device(modes, weights):
    mode_count, cells = modes.shape[1:]
    nx, ny = lax.axis_size("gx"), lax.axis_size("gy")
    width, height = CX * nx, CY * ny
    plane = width * height
    factor = 1.0 / math.sqrt(cells * nx * ny)
    rows = 3 * mode_count
    own_i, own_j = mode_count // nx, mode_count // ny
    pack = max(1, LANES // plane)
    edge = (rows // pack, plane * pack)
    vmem = pl.BlockSpec(memory_space=pltpu.VMEM)
    chips = nx // 2
    near_count, far_count = 6, chips * ny
    return pl.pallas_call(
        functools.partial(kernel, nx, ny, mode_count, width, height, factor),
        out_shape=jax.ShapeDtypeStruct((own_i, own_j, mode_count), jnp.float32),
        in_specs=[vmem, vmem],
        out_specs=vmem,
        scratch_shapes=[
            pltpu.VMEM((rows, cells), jnp.float32),
            pltpu.VMEM((1, cells), jnp.float32),
            pltpu.VMEM((2, *edge), jnp.float32),
            pltpu.VMEM((4, *edge), jnp.float32),
            pltpu.VMEM((nx, 3, own_i, 2 * cells), jnp.float32),
            pltpu.VMEM((3, 3, mode_count, 2 * cells), jnp.float32),
            pltpu.VMEM((2 * mode_count, 6 * cells), jnp.bfloat16),
            pltpu.VMEM((own_i * mode_count, 6 * cells), jnp.bfloat16),
            pltpu.VMEM((own_i * mode_count, 6 * cells), jnp.bfloat16),
            pltpu.VMEM((chips, mode_count, own_i * mode_count), jnp.float32),
            pltpu.VMEM((chips * ny, own_j, own_i * mode_count), jnp.float32),
            pltpu.SemaphoreType.DMA((near_count,)),
            pltpu.SemaphoreType.DMA((near_count,)),
            pltpu.SemaphoreType.DMA((far_count,)),
            pltpu.SemaphoreType.DMA((far_count,)),
        ],
        compiler_params=pltpu.CompilerParams(collective_id=0, has_side_effects=True),
        name="tensor",
    )(modes.reshape(rows, cells), weights.reshape(1, cells))


def solution(mesh):
    return jax.shard_map(
        per_device,
        mesh=mesh,
        in_specs=(P(None, None, ("gx", "gy")), P(("gx", "gy"))),
        out_specs=P("gx", "gy", None),
        check_vma=False,
    )
```

```python
import functools
import math

import jax
import jax.numpy as jnp
from jax import lax
from jax.experimental import pallas as pl
from jax.experimental.pallas import tpu as pltpu
from jax.sharding import PartitionSpec as P

CX = 1
CY = 2
LANES = 128
MESH = pl.DeviceIdType.MESH


def partner_of(gx):
    return gx + 1 - 2 * (gx % 2)


def split(value):
    high = value.astype(jnp.bfloat16)
    low = (value - high.astype(jnp.float32)).astype(jnp.bfloat16)
    return high, low


def kernel(
    nx, ny, modes, width, height, factor,
    x_ref, w_ref, out_ref,
    other_x, other_w, edges, halos, weighted, diffs, field2, high_h, low_h, sums, landed, line, line_in,
    near_send, near_recv, far_send, far_recv, line_send, line_recv,
):
    rows, cells = x_ref.shape
    chips = nx // 2
    devices = nx * ny
    plane = width * height
    pack = max(1, LANES // plane)
    own_i = modes // nx
    own_j = modes // ny
    gx, gy = lax.axis_index("gx"), lax.axis_index("gy")
    core, place = gx % 2, gx // 2
    mate = (partner_of(gx), gy)
    flat = gx * ny + gy

    def beside(step, flat_id):
        other = (flat_id + step + devices) % devices
        return other // ny, other % ny

    def mated(device):
        return partner_of(device[0]), device[1]

    before, after = beside(-1, flat), beside(1, flat)
    mate_flat = mate[0] * ny + gy

    barrier = pltpu.get_barrier_semaphore()
    greeted = [mate, before, after, beside(-1, mate_flat), beside(1, mate_flat)]
    greeted += [((place + s) % chips * 2 + core, gy) for s in range(1, chips)]
    greeted += [(gx, (gy + t) % ny) for t in range(1, ny)]
    for device in greeted:
        pl.semaphore_signal(barrier, inc=1, device_id=device, device_id_type=MESH)

    for edge, start in ((0, 0), (1, cells - plane)):
        if pack == 1:
            edges[edge] = x_ref[:, start : start + plane]
        else:
            base = start // LANES * LANES
            tile = x_ref[:, base : base + LANES]
            part = rows // pack
            lane = lax.broadcasted_iota(jnp.int32, (part, LANES), 1)
            packed = jnp.zeros((part, LANES), jnp.float32)
            for p in range(pack):
                shift = (p * plane - (start - base)) % LANES
                piece = tile[p * part : (p + 1) * part]
                piece = pltpu.roll(piece, shift, 1) if shift else piece
                packed = jnp.where(lane // plane == p, piece, packed)
            edges[edge] = packed

    lane = lax.broadcasted_iota(jnp.int32, (modes, cells), 1)
    at_x, at_y = lane % width, lane // width % height

    def rolled(value, step):
        shift = (-step) % cells
        return pltpu.roll(value, shift, 1) if shift else value

    def plane_of(slot, a):
        if pack == 1:
            tile = halos[slot, a * modes : (a + 1) * modes, :]
        else:
            tiles = []
            part = rows // pack
            narrow = lax.broadcasted_iota(jnp.int32, (8, LANES), 1)
            for r in range(a * modes, (a + 1) * modes, 8):
                p, q = r // part, r % part
                piece = halos[slot, q : q + 8, :]
                full = piece
                for m in range(1, pack):
                    full = jnp.where(narrow // plane == (p + m) % pack, pltpu.roll(piece, m * plane, 1), full)
                tiles.append(full)
            tile = jnp.concatenate(tiles, axis=0)
        return jnp.concatenate([tile] * (cells // tile.shape[1]), axis=1)

    def prepare(which, ref, weight_ref):
        columns = slice(which * cells, (which + 1) * cells)
        weight = weight_ref[...] * factor
        for a in range(3):
            value = ref[a * modes : (a + 1) * modes, :]
            for g in range(nx):
                weighted[g, a, :, columns] = value[g * own_i : (g + 1) * own_i] * weight
            high, low = split(value)
            stage, half = (which, a) if a < 2 else (2, which)
            field2[stage, :modes, half * cells : (half + 1) * cells] = high
            field2[stage, modes:, half * cells : (half + 1) * cells] = low
            up = jnp.where(at_x == width - 1, rolled(value, 1 - width), rolled(value, 1))
            down = jnp.where(at_x == 0, rolled(value, width - 1), rolled(value, -1))
            diffs[a, 0, :, columns] = (up - down) * 0.5
            turn = (height - 1) * width
            up = jnp.where(at_y == height - 1, rolled(value, -turn), rolled(value, width))
            down = jnp.where(at_y == 0, rolled(value, turn), rolled(value, -width))
            diffs[a, 1, :, columns] = (up - down) * 0.5

    def prepare_z(which, ref):
        columns = slice(which * cells, (which + 1) * cells)
        for a in range(3):
            value = ref[a * modes : (a + 1) * modes, :]
            up = jnp.where(lane >= cells - plane, plane_of(2 * which + 1, a), rolled(value, plane))
            down = jnp.where(lane < plane, plane_of(2 * which, a), rolled(value, -plane))
            diffs[a, 2, :, columns] = (up - down) * 0.5

    dims = (((1,), (1,)), ((), ()))

    def block(s, stage):
        group = (place + s) % chips * 2 + core
        for half in range(2):
            b, which = (half, stage) if stage < 2 else (2, half)
            for c in range(0, cells, LANES):
                near_c = slice(which * cells + c, which * cells + c + LANES)
                tiles = [diffs[a, b, :, near_c] for a in range(3)]
                scales = [weighted[group, a, :, near_c] for a in range(3)]
                for i in range(own_i):
                    value = scales[0][i : i + 1] * tiles[0]
                    for a in (1, 2):
                        value = value + scales[a][i : i + 1] * tiles[a]
                    high, low = split(value)
                    place_of = slice(i * modes, (i + 1) * modes), slice(half * cells + c, half * cells + c + LANES)
                    high_h[place_of] = high
                    low_h[place_of] = low
        main = lax.dot_general(field2[stage], high_h[...], dims, preferred_element_type=jnp.float32)
        rest = lax.dot_general(field2[stage, :modes, :], low_h[...], dims, preferred_element_type=jnp.float32)
        value = main[:modes] + (main[modes:] + rest)
        sums[s] = value if stage == 0 else sums[s] + value

    def rows_of(t):
        return pl.ds(pl.multiple_of((gy + t) % ny * own_j, own_j), own_j)

    def far(s, t):
        return pltpu.make_async_remote_copy(
            src_ref=sums.at[s, rows_of(t), :], dst_ref=landed.at[chips - s, t],
            send_sem=far_send.at[s, t], recv_sem=far_recv.at[chips - s, t],
            device_id=((place + s) % chips * 2 + core, gy), device_id_type=MESH,
        )

    def far_in(s, t):
        return pltpu.make_async_remote_copy(
            src_ref=landed.at[s, t], dst_ref=landed.at[s, t],
            send_sem=far_send.at[s, t], recv_sem=far_recv.at[s, t],
            device_id=mate, device_id_type=MESH,
        )

    def along(t):
        return pltpu.make_async_remote_copy(
            src_ref=line.at[t], dst_ref=line_in.at[ny - t],
            send_sem=line_send.at[t], recv_sem=line_recv.at[ny - t],
            device_id=(gx, (gy + t) % ny), device_id_type=MESH,
        )

    def along_in(t):
        return pltpu.make_async_remote_copy(
            src_ref=line_in.at[t], dst_ref=line_in.at[t],
            send_sem=line_send.at[t], recv_sem=line_recv.at[t],
            device_id=mate, device_id_type=MESH,
        )

    def sweep(stage):
        def body(s, carry):
            block(s, stage)
            return carry

        lax.fori_loop(0, chips, body, 0)

    order = list(range(ny - 1, 0, -1)) + [0]
    prepare(0, x_ref, w_ref)
    sweep(0)
    pl.semaphore_wait(barrier, len(greeted))

    def near(index, src, dst, device):
        return pltpu.make_async_remote_copy(
            src_ref=src, dst_ref=dst, send_sem=near_send.at[index], recv_sem=near_recv.at[index],
            device_id=device, device_id_type=MESH,
        )

    copies = [
        near(0, edges.at[1], halos.at[0], after),
        near(1, edges.at[0], halos.at[1], before),
        near(2, edges.at[1], halos.at[2], mated(after)),
        near(3, edges.at[0], halos.at[3], mated(before)),
        near(4, w_ref, other_w, mate),
        near(5, x_ref, other_x, mate),
    ]
    for copy in copies:
        copy.start()

    copies[4].wait_recv()
    copies[5].wait_recv()
    prepare(1, other_x, other_w)
    sweep(1)
    for copy in copies[:4]:
        copy.wait_recv()
    prepare_z(0, x_ref)
    prepare_z(1, other_x)
    for s in range(chips - 1, 0, -1):
        block(s, 2)
        for t in order:
            far(s, t).start()
    block(0, 2)
    for t in order:
        total = sums[0, rows_of(t), :]
        for s in range(1, chips):
            far_in(s, t).wait_recv()
            total = total + landed[s, t]
        line[t] = total
        if t:
            along(t).start()
    total = line[0]
    for t in range(1, ny):
        along_in(t).wait_recv()
        total = total + line_in[t]
    for i in range(own_i):
        out_ref[i] = total[:, i * modes : (i + 1) * modes]
    for copy in copies:
        copy.wait_send()
    for s in range(1, chips):
        for t in range(ny):
            far(s, t).wait_send()
    for t in range(1, ny):
        along(t).wait_send()


def per_device(modes, weights):
    mode_count, cells = modes.shape[1:]
    nx, ny = lax.axis_size("gx"), lax.axis_size("gy")
    width, height = CX * nx, CY * ny
    plane = width * height
    factor = 1.0 / math.sqrt(cells * nx * ny)
    rows = 3 * mode_count
    own_i, own_j = mode_count // nx, mode_count // ny
    pack = max(1, LANES // plane)
    edge = (rows // pack, plane * pack)
    vmem = pl.BlockSpec(memory_space=pltpu.VMEM)
    chips = nx // 2
    near_count = 6
    return pl.pallas_call(
        functools.partial(kernel, nx, ny, mode_count, width, height, factor),
        out_shape=jax.ShapeDtypeStruct((own_i, own_j, mode_count), jnp.float32),
        in_specs=[vmem, vmem],
        out_specs=vmem,
        scratch_shapes=[
            pltpu.VMEM((rows, cells), jnp.float32),
            pltpu.VMEM((1, cells), jnp.float32),
            pltpu.VMEM((2, *edge), jnp.float32),
            pltpu.VMEM((4, *edge), jnp.float32),
            pltpu.VMEM((nx, 3, own_i, 2 * cells), jnp.float32),
            pltpu.VMEM((3, 3, mode_count, 2 * cells), jnp.float32),
            pltpu.VMEM((3, 2 * mode_count, 2 * cells), jnp.bfloat16),
            pltpu.VMEM((own_i * mode_count, 2 * cells), jnp.bfloat16),
            pltpu.VMEM((own_i * mode_count, 2 * cells), jnp.bfloat16),
            pltpu.VMEM((chips, mode_count, own_i * mode_count), jnp.float32),
            pltpu.VMEM((chips, ny, own_j, own_i * mode_count), jnp.float32),
            pltpu.VMEM((ny, own_j, own_i * mode_count), jnp.float32),
            pltpu.VMEM((ny, own_j, own_i * mode_count), jnp.float32),
            pltpu.SemaphoreType.DMA((near_count,)),
            pltpu.SemaphoreType.DMA((near_count,)),
            pltpu.SemaphoreType.DMA((chips, ny)),
            pltpu.SemaphoreType.DMA((chips, ny)),
            pltpu.SemaphoreType.DMA((ny,)),
            pltpu.SemaphoreType.DMA((ny,)),
        ],
        compiler_params=pltpu.CompilerParams(collective_id=0, has_side_effects=True),
        name="tensor",
    )(modes.reshape(rows, cells), weights.reshape(1, cells))


def solution(mesh):
    return jax.shard_map(
        per_device,
        mesh=mesh,
        in_specs=(P(None, None, ("gx", "gy")), P(("gx", "gy"))),
        out_specs=P("gx", "gy", None),
        check_vma=False,
    )
```

```python
import functools
import math

import jax
import jax.numpy as jnp
from jax import lax
from jax.experimental import pallas as pl
from jax.experimental.pallas import tpu as pltpu
from jax.sharding import PartitionSpec as P

CX = 1
CY = 2
LANES = 128
MESH = pl.DeviceIdType.MESH


def partner_of(gx):
    return gx + 1 - 2 * (gx % 2)


def split(value):
    high = value.astype(jnp.bfloat16)
    low = (value - high.astype(jnp.float32)).astype(jnp.bfloat16)
    return high, low


def kernel(
    nx, ny, modes, width, height, factor,
    x_ref, w_ref, out_ref,
    other_x, other_w, edges, halos, weighted, diffs, field2, high_h, low_h, sums, landed, line, line_in,
    near_send, near_recv, far_send, far_recv, line_send, line_recv,
):
    rows, cells = x_ref.shape
    chips = nx // 2
    devices = nx * ny
    plane = width * height
    pack = max(1, LANES // plane)
    own_i = modes // nx
    own_j = modes // ny
    gx, gy = lax.axis_index("gx"), lax.axis_index("gy")
    core, place = gx % 2, gx // 2
    mate = (partner_of(gx), gy)
    minor = 2 - chips % 2
    major = chips // minor

    def shifted(s):
        return (place // minor + s // minor) % major * minor + (place % minor + s % minor) % minor

    def mirrored(s):
        return -(s // minor) % major * minor + -(s % minor) % minor

    flat = gx * ny + gy

    def beside(step, flat_id):
        other = (flat_id + step + devices) % devices
        return other // ny, other % ny

    before, after = beside(-1, flat), beside(1, flat)

    barrier = pltpu.get_barrier_semaphore()
    greeted = [mate, before, after]
    greeted += [(shifted(s) * 2 + core, gy) for s in range(1, chips) if s < minor or s % minor == 0]
    greeted += [(gx, (gy + t) % ny) for t in range(1, ny)]
    for device in greeted:
        pl.semaphore_signal(barrier, inc=1, device_id=device, device_id_type=MESH)

    for edge, start in ((0, 0), (1, cells - plane)):
        if pack == 1:
            edges[edge] = x_ref[:, start : start + plane]
        else:
            base = start // LANES * LANES
            tile = x_ref[:, base : base + LANES]
            part = rows // pack
            lane = lax.broadcasted_iota(jnp.int32, (part, LANES), 1)
            packed = jnp.zeros((part, LANES), jnp.float32)
            for p in range(pack):
                shift = (p * plane - (start - base)) % LANES
                piece = tile[p * part : (p + 1) * part]
                piece = pltpu.roll(piece, shift, 1) if shift else piece
                packed = jnp.where(lane // plane == p, piece, packed)
            edges[edge] = packed

    lane = lax.broadcasted_iota(jnp.int32, (modes, cells), 1)
    at_x, at_y = lane % width, lane // width % height

    def rolled(value, step):
        shift = (-step) % cells
        return pltpu.roll(value, shift, 1) if shift else value

    def plane_of(slot, a):
        if pack == 1:
            tile = halos[slot, a * modes : (a + 1) * modes, :]
        else:
            tiles = []
            part = rows // pack
            narrow = lax.broadcasted_iota(jnp.int32, (8, LANES), 1)
            for r in range(a * modes, (a + 1) * modes, 8):
                p, q = r // part, r % part
                piece = halos[slot, q : q + 8, :]
                full = piece
                for m in range(1, pack):
                    full = jnp.where(narrow // plane == (p + m) % pack, pltpu.roll(piece, m * plane, 1), full)
                tiles.append(full)
            tile = jnp.concatenate(tiles, axis=0)
        return jnp.concatenate([tile] * (cells // tile.shape[1]), axis=1)

    def prepare(which, ref, weight_ref):
        columns = slice(which * cells, (which + 1) * cells)
        weight = weight_ref[...] * factor
        for a in range(3):
            value = ref[a * modes : (a + 1) * modes, :]
            for g in range(nx):
                weighted[g, a, :, columns] = value[g * own_i : (g + 1) * own_i] * weight
            high, low = split(value)
            stage, half = (which, a) if a < 2 else (2, which)
            field2[stage, :modes, half * cells : (half + 1) * cells] = high
            field2[stage, modes:, half * cells : (half + 1) * cells] = low
            up = jnp.where(at_x == width - 1, rolled(value, 1 - width), rolled(value, 1))
            down = jnp.where(at_x == 0, rolled(value, width - 1), rolled(value, -1))
            diffs[a, 0, :, columns] = (up - down) * 0.5
            turn = (height - 1) * width
            up = jnp.where(at_y == height - 1, rolled(value, -turn), rolled(value, width))
            down = jnp.where(at_y == 0, rolled(value, turn), rolled(value, -width))
            diffs[a, 1, :, columns] = (up - down) * 0.5

    def prepare_z(which, ref):
        columns = slice(which * cells, (which + 1) * cells)
        for a in range(3):
            value = ref[a * modes : (a + 1) * modes, :]
            up = jnp.where(lane >= cells - plane, plane_of(2 * which + 1, a), rolled(value, plane))
            down = jnp.where(lane < plane, plane_of(2 * which, a), rolled(value, -plane))
            diffs[a, 2, :, columns] = (up - down) * 0.5

    dims = (((1,), (1,)), ((), ()))

    def block(s, stage):
        group = shifted(s) * 2 + core
        for half in range(2):
            b, which = (half, stage) if stage < 2 else (2, half)
            for c in range(0, cells, LANES):
                near_c = slice(which * cells + c, which * cells + c + LANES)
                tiles = [diffs[a, b, :, near_c] for a in range(3)]
                scales = [weighted[group, a, :, near_c] for a in range(3)]
                for i in range(own_i):
                    value = scales[0][i : i + 1] * tiles[0]
                    for a in (1, 2):
                        value = value + scales[a][i : i + 1] * tiles[a]
                    high, low = split(value)
                    place_of = slice(i * modes, (i + 1) * modes), slice(half * cells + c, half * cells + c + LANES)
                    high_h[place_of] = high
                    low_h[place_of] = low
        main = lax.dot_general(field2[stage], high_h[...], dims, preferred_element_type=jnp.float32)
        rest = lax.dot_general(field2[stage, :modes, :], low_h[...], dims, preferred_element_type=jnp.float32)
        value = main[:modes] + (main[modes:] + rest)
        sums[s] = value if stage == 0 else sums[s] + value

    def rows_of(t):
        return pl.ds(pl.multiple_of((gy + t) % ny * own_j, own_j), own_j)

    def along_minor(s, t):
        return s % minor > 0 and (s < minor or t % 2 == 0)

    def far(s, t):
        if along_minor(s, t):
            hop, slot = s % minor, s
        else:
            hop = s // minor * minor
            slot = mirrored(hop) + s % minor
        return pltpu.make_async_remote_copy(
            src_ref=sums.at[s, rows_of(t), :], dst_ref=landed.at[slot, t],
            send_sem=far_send.at[s, t], recv_sem=far_recv.at[slot, t],
            device_id=(shifted(hop) * 2 + core, gy), device_id_type=MESH,
        )

    def far_in(s, t):
        return pltpu.make_async_remote_copy(
            src_ref=landed.at[s, t], dst_ref=landed.at[s, t],
            send_sem=far_send.at[s, t], recv_sem=far_recv.at[s, t],
            device_id=mate, device_id_type=MESH,
        )

    def along(t):
        return pltpu.make_async_remote_copy(
            src_ref=line.at[t], dst_ref=line_in.at[ny - t],
            send_sem=line_send.at[t], recv_sem=line_recv.at[ny - t],
            device_id=(gx, (gy + t) % ny), device_id_type=MESH,
        )

    def along_in(t):
        return pltpu.make_async_remote_copy(
            src_ref=line_in.at[t], dst_ref=line_in.at[t],
            send_sem=line_send.at[t], recv_sem=line_recv.at[t],
            device_id=mate, device_id_type=MESH,
        )

    def sweep(stage):
        def body(s, carry):
            block(s, stage)
            return carry

        lax.fori_loop(0, chips, body, 0)

    order = list(range(ny - 1, 0, -1)) + [0]
    prepare(0, x_ref, w_ref)
    sweep(0)
    pl.semaphore_wait(barrier, len(greeted))

    def near(index, src, dst, device):
        return pltpu.make_async_remote_copy(
            src_ref=src, dst_ref=dst, send_sem=near_send.at[index], recv_sem=near_recv.at[index],
            device_id=device, device_id_type=MESH,
        )

    copies = [
        near(0, edges.at[1], halos.at[0], after),
        near(1, edges.at[0], halos.at[1], before),
        near(2, halos.at[0], halos.at[2], mate),
        near(3, halos.at[1], halos.at[3], mate),
        near(4, w_ref, other_w, mate),
        near(5, x_ref, other_x, mate),
    ]
    for index in (0, 1, 4, 5):
        copies[index].start()

    copies[4].wait_recv()
    copies[5].wait_recv()
    prepare(1, other_x, other_w)
    sweep(1)
    for index in (0, 1):
        copies[index].wait_recv()
        copies[index + 2].start()
    prepare_z(0, x_ref)
    for index in (2, 3):
        copies[index].wait_recv()
    prepare_z(1, other_x)
    cross = [s for s in range(chips) if s % minor and s >= minor]
    inner = list(range(1, minor))
    outer = [s for s in range(minor, chips, minor)]

    def waits_for(s, t):
        if minor == 1:
            return []
        if t % 2 == 0:
            return [s + 1] if s in outer else []
        return cross if s in inner else []

    for s in cross + inner + outer:
        block(s, 2)
        for t in order:
            if not waits_for(s, t):
                far(s, t).start()
    block(0, 2)
    for t in order:
        for s in inner + outer:
            if waits_for(s, t):
                value = sums[s, rows_of(t), :]
                for source in waits_for(s, t):
                    far_in(source, t).wait_recv()
                    value = value + landed[source, t]
                sums[s, rows_of(t), :] = value
                far(s, t).start()
    for t in order:
        total = sums[0, rows_of(t), :]
        for s in inner + outer:
            far_in(s, t).wait_recv()
            total = total + landed[s, t]
        line[t] = total
        if t:
            along(t).start()
    total = line[0]
    for t in range(1, ny):
        along_in(t).wait_recv()
        total = total + line_in[t]
    for i in range(own_i):
        out_ref[i] = total[:, i * modes : (i + 1) * modes]
    for copy in copies:
        copy.wait_send()
    for s in range(1, chips):
        for t in range(ny):
            far(s, t).wait_send()
    for t in range(1, ny):
        along(t).wait_send()


def per_device(modes, weights):
    mode_count, cells = modes.shape[1:]
    nx, ny = lax.axis_size("gx"), lax.axis_size("gy")
    width, height = CX * nx, CY * ny
    plane = width * height
    factor = 1.0 / math.sqrt(cells * nx * ny)
    rows = 3 * mode_count
    own_i, own_j = mode_count // nx, mode_count // ny
    pack = max(1, LANES // plane)
    edge = (rows // pack, plane * pack)
    vmem = pl.BlockSpec(memory_space=pltpu.VMEM)
    chips = nx // 2
    near_count = 6
    return pl.pallas_call(
        functools.partial(kernel, nx, ny, mode_count, width, height, factor),
        out_shape=jax.ShapeDtypeStruct((own_i, own_j, mode_count), jnp.float32),
        in_specs=[vmem, vmem],
        out_specs=vmem,
        scratch_shapes=[
            pltpu.VMEM((rows, cells), jnp.float32),
            pltpu.VMEM((1, cells), jnp.float32),
            pltpu.VMEM((2, *edge), jnp.float32),
            pltpu.VMEM((4, *edge), jnp.float32),
            pltpu.VMEM((nx, 3, own_i, 2 * cells), jnp.float32),
            pltpu.VMEM((3, 3, mode_count, 2 * cells), jnp.float32),
            pltpu.VMEM((3, 2 * mode_count, 2 * cells), jnp.bfloat16),
            pltpu.VMEM((own_i * mode_count, 2 * cells), jnp.bfloat16),
            pltpu.VMEM((own_i * mode_count, 2 * cells), jnp.bfloat16),
            pltpu.VMEM((chips, mode_count, own_i * mode_count), jnp.float32),
            pltpu.VMEM((chips, ny, own_j, own_i * mode_count), jnp.float32),
            pltpu.VMEM((ny, own_j, own_i * mode_count), jnp.float32),
            pltpu.VMEM((ny, own_j, own_i * mode_count), jnp.float32),
            pltpu.SemaphoreType.DMA((near_count,)),
            pltpu.SemaphoreType.DMA((near_count,)),
            pltpu.SemaphoreType.DMA((chips, ny)),
            pltpu.SemaphoreType.DMA((chips, ny)),
            pltpu.SemaphoreType.DMA((ny,)),
            pltpu.SemaphoreType.DMA((ny,)),
        ],
        compiler_params=pltpu.CompilerParams(collective_id=0, has_side_effects=True),
        name="tensor",
    )(modes.reshape(rows, cells), weights.reshape(1, cells))


def solution(mesh):
    return jax.shard_map(
        per_device,
        mesh=mesh,
        in_specs=(P(None, None, ("gx", "gy")), P(("gx", "gy"))),
        out_specs=P("gx", "gy", None),
        check_vma=False,
    )
```
